32 devices in a mesh: groups: 2 (over x), seq: 16 (over z, y, core).
Axes of the slice: x: 2, y: 2, z: 4, core: 2. Of those that a mesh axis runs over, the one named last changes fastest.
Arguments:
- queries: bfloat16 [4096, 2560], P(('groups', 'seq')), parts along dimension 0, may hold values from -12 to 12
- key_vectors: bfloat16 [4096, 2560], P(('groups', 'seq')), parts along dimension 0, may hold values from -6 to 6
- value_vectors: bfloat16 [4096, 2560], P(('groups', 'seq')), parts along dimension 0, may hold values from -6 to 6
- step_sizes: float32 [4096, 8], P(('groups', 'seq')), parts along dimension 0, may hold values from 0.02 to 0.3
- fast_weights: float32 [320, 7680], P('seq'), may hold values from -20 to 20
- fast_gain: float32 [2560], replicated, may hold values from 0.25 to 1.75
- window_gain: float32 [2560], replicated, may hold values from 0.25 to 1.75
Outputs:
- layer_out: bfloat16 [4096, 2560], P(('groups', 'seq')), parts along dimension 0
- new_weights: float32 [640, 7680], P(('groups', 'seq')), parts along dimension 0
- momentum: float32 [640, 7680], P(('groups', 'seq')), parts along dimension 0
The draws below stay inside these ranges and needn't reach their ends.
There are 2 independent parts, one for each index of `groups`. The reference program is written for one: setup_inputs(seed, part) draws one part's arguments, and reference() takes and returns one part's arrays. A program takes and returns all parts, laid end to end along the dimension named above; an argument that names none is the same for every part. Nothing has to cross between parts.
All inputs are finite; a program needn't handle non-finite values.
Results may differ from the reference program's by a relative error of at most 0.0066.
Values may be sent and summed in bfloat16 or wider, within the bound.
A program may use at most 128 MiB of HBM per device.

```python
import math
import jax
import jax.numpy as jnp
from jax import lax

H = 8
DH = 320
WINDOW = 1024
BLOCK = 2048


def draw_queries(key, part):
    return jnp.clip(jax.random.normal(jax.random.fold_in(key, 1), (BLOCK, H * DH)), -6.0, 6.0).astype(jnp.bfloat16)


def draw_key_vectors(key, part):
    return jnp.clip(jax.random.normal(jax.random.fold_in(key, 2), (BLOCK, H * DH)), -6.0, 6.0).astype(jnp.bfloat16)


def draw_fast_weights(key, part):
    columns = 3 * H * DH
    rising = (3.0 ** (jnp.arange(DH, dtype=jnp.float32) / (DH - 1)))[:, None]
    entries = jnp.clip(jax.random.normal(jax.random.fold_in(key, 1), (DH, columns)), -4.0, 4.0)
    row_factor = 0.5 * rising * jnp.exp(jax.random.uniform(jax.random.fold_in(key, 2), (DH, 1), minval=-0.7, maxval=0.7))
    col_factor = jnp.exp(jax.random.uniform(jax.random.fold_in(key, 3), (1, columns), minval=-1.15, maxval=1.15))
    return jnp.clip(entries * row_factor * col_factor, -20.0, 20.0)


def shard_levels(rng, shape, shards, smallest, largest):
    def one(position, parts):
        steps = jax.random.uniform(jax.random.fold_in(jax.random.fold_in(rng, 6), position), (parts,), jnp.float32, smallest / len(shards), largest / len(shards))
        return jnp.repeat(jnp.exp(steps), shape[position] // parts).reshape((-1,) + (1,) * (len(shape) - position - 1))

    factor_of = one(*shards[0])
    for cut in shards[1:]:
        factor_of = factor_of * one(*cut)
    return factor_of


def gaussian(key, dims, deviation, reach, split=(), kind=jnp.bfloat16):
    values = deviation * jax.random.normal(key, dims, jnp.float32)
    if split:
        values = values * shard_levels(key, dims, split, -0.22, 0.18)
    return jnp.clip(values, -reach, reach).astype(kind)


def setup_inputs(seed: int = 0, part: int = 0) -> dict:
    key_list = jax.random.split(jax.random.key(seed), 8)
    own_keys = jax.random.split(jax.random.fold_in(key_list[7], part), 8)
    return {
        "queries": draw_queries(jax.random.fold_in(jax.random.fold_in(key_list[7], part), 71), part),
        "key_vectors": draw_key_vectors(jax.random.fold_in(jax.random.fold_in(key_list[7], part), 71), part),
        "value_vectors": gaussian(own_keys[2], (BLOCK, H * DH), 1.0, 6.0, ((0, 16),)),
        "step_sizes": jnp.clip(jnp.exp(math.log(0.3) - 2.7080503 * jax.random.uniform(own_keys[3], (BLOCK, H), jnp.float32) ** shard_levels(own_keys[3], (BLOCK, H), ((0, 16),), -0.2, 0.2)), 0.02, 0.3),
        "fast_weights": draw_fast_weights(jax.random.fold_in(key_list[7], 71), part),
        "fast_gain": jnp.clip(1.0 + 0.15 * jax.random.normal(key_list[5], (H * DH,), jnp.float32), 0.25, 1.75),
        "window_gain": jnp.clip(1.0 + 0.15 * jax.random.normal(key_list[6], (H * DH,), jnp.float32), 0.25, 1.75),
    }


def normalize(field, gain_row):
    mean_sq = lax.optimization_barrier(jnp.mean(field * field, axis=-1, keepdims=True))
    return field * lax.rsqrt(mean_sq + 1e-05) * gain_row

def silu_slope(gate):
    sigma = jax.nn.sigmoid(gate)
    return sigma * (1.0 + gate * (1.0 - sigma))

def reference(queries, key_vectors, value_vectors, step_sizes, fast_weights, fast_gain, window_gain):
    score_scale = 1.0 / math.sqrt(DH)
    copies = fast_weights.astype(jnp.bfloat16).reshape(DH, 3, H, DH)
    w_first = copies[:, 0]
    w_third = copies[:, 1]
    w_second = copies[:, 2]
    query_heads = queries.reshape(BLOCK, H, DH)
    key_heads = key_vectors.reshape(BLOCK, H, DH)
    value_heads = value_vectors.reshape(BLOCK, H, DH)

    def project(inputs, matrix):
        return jnp.einsum('thr,rhc->thc', inputs.astype(jnp.float32), matrix.astype(jnp.float32)) * score_scale
    gate_query = project(query_heads, w_first)
    up_query = project(query_heads, w_third)
    hidden_query = (jax.nn.silu(gate_query) * up_query).astype(jnp.bfloat16)
    fast_part = normalize(project(hidden_query, w_second), fast_gain.reshape(H, DH))
    padding = jnp.zeros((WINDOW, H * DH), jnp.bfloat16)
    padded_keys = jnp.concatenate([padding, key_vectors], axis=0)
    padded_values = jnp.concatenate([padding, value_vectors], axis=0)

    def window_block(block_index):
        begin = block_index * WINDOW
        query_block = lax.dynamic_slice_in_dim(queries, begin, WINDOW, 0).reshape(WINDOW, H, DH)
        key_block = lax.dynamic_slice_in_dim(padded_keys, begin, 2 * WINDOW, 0).reshape(2 * WINDOW, H, DH)
        value_block = lax.dynamic_slice_in_dim(padded_values, begin, 2 * WINDOW, 0).reshape(2 * WINDOW, H, DH)
        query_pos = begin + jnp.arange(WINDOW, dtype=jnp.int32)
        key_pos = begin - WINDOW + jnp.arange(2 * WINDOW, dtype=jnp.int32)
        distance = query_pos[:, None] - key_pos[None, :]
        allowed = (distance >= 0) & (distance < WINDOW) & (key_pos[None, :] >= 0)
        scores = jnp.einsum('qhd,khd->hqk', query_block.astype(jnp.float32), key_block.astype(jnp.float32)) * score_scale
        scores = jnp.where(allowed[None], scores, -jnp.inf)
        row_max = lax.optimization_barrier(jnp.max(scores, axis=-1, keepdims=True))
        weights = jnp.exp(scores - row_max)
        attention_probs = (weights / lax.optimization_barrier(jnp.sum(weights, axis=-1, keepdims=True))).astype(jnp.bfloat16)
        return jnp.einsum('hqk,khd->qhd', attention_probs.astype(jnp.float32), value_block.astype(jnp.float32))
    attended = lax.map(window_block, jnp.arange(BLOCK // WINDOW, dtype=jnp.int32)).reshape(BLOCK, H, DH)
    window_part = normalize(attended, window_gain.reshape(H, DH))
    layer_out = (fast_part + window_part).astype(jnp.bfloat16).reshape(BLOCK, H * DH)
    gate_key = project(key_heads, w_first)
    up_key = project(key_heads, w_third)
    hidden_key = (jax.nn.silu(gate_key) * up_key).astype(jnp.bfloat16)
    target = (-step_sizes[:, :, None] * value_heads.astype(jnp.float32)).astype(jnp.bfloat16)
    back_hidden = jnp.einsum('thc,rhc->thr', target.astype(jnp.float32), w_second.astype(jnp.float32)) * score_scale
    grad_gate = (back_hidden * up_key * silu_slope(gate_key)).astype(jnp.bfloat16)
    grad_up = (back_hidden * jax.nn.silu(gate_key)).astype(jnp.bfloat16)
    key_float = key_heads.astype(jnp.float32)
    first = jnp.einsum('thr,thc->rhc', key_float, grad_gate.astype(jnp.float32))
    third = jnp.einsum('thr,thc->rhc', key_float, grad_up.astype(jnp.float32))
    second = jnp.einsum('thr,thc->rhc', hidden_key.astype(jnp.float32), target.astype(jnp.float32))
    momentum = jnp.stack([first, third, second], axis=1).reshape(DH, 3 * H * DH) * score_scale
    moved = fast_weights - momentum
    old_sum = lax.optimization_barrier(jnp.sum(fast_weights * fast_weights, axis=0))
    new_sum = lax.optimization_barrier(jnp.sum(moved * moved, axis=0))
    new_weights = moved * jnp.sqrt((old_sum + 1e-06) / (new_sum + 1e-06))
    return (layer_out, new_weights, momentum)
```

```python
import functools
import math

import jax
import jax.numpy as jnp
from jax import lax
from jax.experimental import pallas as pl
from jax.experimental.pallas import tpu as pltpu
from jax.sharding import PartitionSpec as P

WINDOW = 1024
LANES = 128
F32 = jnp.float32
BF16 = jnp.bfloat16


def dot(a, b):
    return jnp.dot(a, b, preferred_element_type=F32)


def dot_nt(a, b):
    return lax.dot_general(a, b, (((1,), (1,)), ((), ())), preferred_element_type=F32)


def dot_tn(a, b):
    return lax.dot_general(a, b, (((0,), (0,)), ((), ())), preferred_element_type=F32)


def kernel(
    n, heads, width,
    q_in, k_in, v_in, step_in, w_in, gains,
    out, g_out, scale_out,
    qb, kb, vb, stb, wb, wfull, kn, hid, tgt, gg, gu,
    gstage, ginc, gsend, sums, sinc, scale_send, ostage,
    s_in, r_q, r_k, r_v, r_st, r_w,
    s_wf, s_kf, s_vf,
    s_gp, r_gp, s_sp, r_sp, s_g, r_g, s_sc, r_sc, s_o, r_o,
):
    group = n // heads
    rows = width // n
    span = heads * LANES
    scale = 1.0 / math.sqrt(width)
    me = lax.axis_index("seq")
    head = me // group
    member = me % group
    block_member = me // heads
    block_slot = me % heads

    def remote(src, dst, send, recv, device):
        return pltpu.make_async_remote_copy(
            src_ref=src, dst_ref=dst, send_sem=send, recv_sem=recv,
            device_id={"seq": device}, device_id_type=pl.DeviceIdType.MESH,
        )

    barrier = pltpu.get_barrier_semaphore()
    for step in range(1, n):
        pl.semaphore_signal(
            barrier, inc=1, device_id={"seq": lax.rem(me + step, n)},
            device_id_type=pl.DeviceIdType.MESH,
        )
    pl.semaphore_wait(barrier, n - 1)

    def lanes(slot):
        return pl.ds(pl.multiple_of(slot * LANES, LANES), LANES)

    def head_rows(which):
        return pl.ds(pl.multiple_of(which * width, 64), width)

    is_self = block_member == member
    pending = []
    maybe = []

    def spread(src_of, dst, recv, kind):
        for step in range(heads):
            which = lax.rem(head + step, heads)
            device = which * group + block_member
            src = src_of(which)
            copy = remote(src, dst, s_in.at[kind, step], recv, device)
            if step == 0:
                @pl.when(is_self)
                def _():
                    pltpu.make_async_copy(src, dst, recv).start()

                @pl.when(jnp.logical_not(is_self))
                def _():
                    copy.start()
                maybe.append(copy)
            else:
                copy.start()
                pending.append(copy)

    for step in range(heads):
        which = lax.rem(head + step, heads)
        device = which * group + member
        if step == 0:
            pltpu.make_async_copy(w_in.at[which], wb.at[me], r_w.at[me]).start()
        else:
            copy = remote(w_in.at[which], wb.at[me], s_in.at[4, step], r_w.at[me], device)
            copy.start()
            pending.append(copy)
    own = heads + block_slot
    spread(lambda w: k_in.at[head_rows(w), :], kb.at[:, lanes(own)], r_k.at[own], 0)
    spread(lambda w: v_in.at[head_rows(w), :], vb.at[:, lanes(own)], r_v.at[own], 1)
    spread(lambda w: step_in, stb.at[block_slot], r_st.at[block_slot], 2)
    spread(lambda w: q_in.at[head_rows(w), :], qb.at[:, lanes(block_slot)], r_q.at[block_slot], 3)

    @pl.when(member == 0)
    def _():
        kb[:, :span] = jnp.zeros((width, span), BF16)
        vb[:, :span] = jnp.zeros((width, span), BF16)

    def landed(ref, sem):
        pltpu.make_async_copy(ref, ref, sem).wait()

    for i in range(heads):
        slot = member + group * i
        landed(wb.at[slot], r_w.at[slot])
        for d in range(1, group):
            copy = remote(
                wb.at[slot], wb.at[slot], s_wf.at[i, d - 1], r_w.at[slot],
                head * group + lax.rem(member + d, group),
            )
            copy.start()
            pending.append(copy)

    forwards = []
    for i in range(heads):
        a, b = (heads + i) * LANES, i * LANES
        for buf, send, recv in ((kb, s_kf, r_k), (vb, s_vf, r_v)):
            landed(buf.at[:, pl.ds(a, LANES)], recv.at[heads + i])
            copy = remote(
                buf.at[:, pl.ds(a, LANES)], buf.at[:, pl.ds(b, LANES)], send.at[i], recv.at[i], me + 1
            )
            forwards.append(copy)

            @pl.when(member < group - 1)
            def _():
                copy.start()
    for d in range(1, group):
        for i in range(heads):
            slot = lax.rem(member + d, group) + group * i
            landed(wb.at[slot], r_w.at[slot])
    for s in range(n):
        piece = wb[s].astype(F32)
        for m in range(3):
            wfull[m, s * rows : (s + 1) * rows, :] = piece[m * rows : (m + 1) * rows, :]
    for i in range(heads):
        landed(stb.at[i], r_st.at[i])

    w1 = wfull[0].astype(BF16)
    w3 = wfull[1].astype(BF16)
    w2 = wfull[2].astype(BF16)

    for i in range(heads):
        here = pl.ds(span + i * LANES, LANES)
        there = pl.ds(i * LANES, LANES)
        tgt[:, there] = (-stb[i, pl.ds(head, 1), :] * vb[:, here].astype(F32)).astype(BF16)
    chunk = 2 * LANES

    def grad_chunk(c, carry):
        here = pl.ds(pl.multiple_of(span + c * chunk, chunk), chunk)
        there = pl.ds(pl.multiple_of(c * chunk, chunk), chunk)
        keys = kb[:, here]
        gate = dot_tn(w1, keys) * scale
        up = dot_tn(w3, keys) * scale
        back = dot(w2, tgt[:, there]) * scale
        sigma = jax.nn.sigmoid(gate)
        silu = gate * sigma
        hid[:, there] = (silu * up).astype(BF16)
        gg[:, there] = (back * up * (sigma * (1.0 + gate * (1.0 - sigma)))).astype(BF16)
        gu[:, there] = (back * silu).astype(BF16)
        return carry

    lax.fori_loop(0, span // chunk, grad_chunk, 0)
    own_keys = kb[:, span:]
    for m, (left, right) in enumerate(((own_keys, gg), (own_keys, gu), (hid[...], tgt))):
        grad = dot_nt(left, right[...]) * scale
        for s in range(n):
            gstage[s % group, s // group, m * rows : (m + 1) * rows, :] = grad[s * rows : (s + 1) * rows, :]

    for d in range(1, group):
        other = lax.rem(member + d, group)
        copy = remote(
            gstage.at[other], ginc.at[d - 1], s_gp.at[d - 1], r_gp.at[d - 1], head * group + other
        )
        copy.start()
        pending.append(copy)

    @pl.when(member > 0)
    def _():
        for i in range(heads):
            landed(kb.at[:, pl.ds(i * LANES, LANES)], r_k.at[i])
            landed(vb.at[:, pl.ds(i * LANES, LANES)], r_v.at[i])

    def flip(c, carry):
        at = pl.ds(pl.multiple_of(c * LANES, LANES), LANES)
        kn[at, :] = kb[:, at].T
        return carry

    lax.fori_loop(0, 2 * heads, flip, 0)

    for d in range(1, group):
        landed(ginc.at[d - 1], r_gp.at[d - 1])
    sums[...] = jnp.zeros_like(sums)

    def add_up(i, carry):
        total = gstage[member, i]
        for d in range(1, group):
            total = total + ginc[d - 1, i]
        gsend[i] = total.astype(BF16)
        weight = wb[member + group * i].astype(F32)
        moved = weight - total
        for m in range(3):
            part = slice(m * rows, (m + 1) * rows)
            old = weight[part, :]
            new = moved[part, :]
            sums[m : m + 1, :] += jnp.sum(old * old, axis=0, keepdims=True)
            sums[4 + m : 5 + m, :] += jnp.sum(new * new, axis=0, keepdims=True)
        return carry

    lax.fori_loop(0, heads, add_up, 0)
    for d in range(1, group):
        copy = remote(
            sums, sinc.at[d - 1], s_sp.at[d - 1], r_sp.at[d - 1],
            head * group + lax.rem(member + d, group),
        )
        copy.start()
        pending.append(copy)

    for i in range(heads):
        landed(qb.at[:, pl.ds(i * LANES, LANES)], r_q.at[i])

    reach = WINDOW + chunk
    key_at = lax.broadcasted_iota(jnp.int32, (reach, chunk), 0)
    query_at = lax.broadcasted_iota(jnp.int32, (reach, chunk), 1)
    distance = WINDOW + query_at - key_at
    in_window = (distance >= 0) & (distance < WINDOW)
    first_key = jnp.where(member == 0, span, 0)

    def normalize(field, gain):
        mean_sq = jnp.mean(field * field, axis=0, keepdims=True)
        return field * lax.rsqrt(mean_sq + 1e-05) * gain

    outs = []

    def attend(c):
        start = c * chunk
        query = qb[:, pl.ds(start, chunk)]
        scores = dot(kn[pl.ds(start, reach), :], query) * scale
        allowed = in_window & (key_at + start >= first_key)
        scores = jnp.where(allowed, scores, -1e30)
        weights = jnp.exp(scores - jnp.max(scores, axis=0, keepdims=True))
        probs = (weights / jnp.sum(weights, axis=0, keepdims=True)).astype(BF16)
        attended = dot(vb[:, pl.ds(start, reach)], probs)
        window_part = normalize(attended, gains[1, :, 0:1])
        gate = dot_tn(w1, query) * scale
        up = dot_tn(w3, query) * scale
        hidden = (gate * jax.nn.sigmoid(gate) * up).astype(BF16)
        fast_part = normalize(dot_tn(w2, hidden) * scale, gains[0, :, 0:1])
        result = (fast_part + window_part).astype(BF16)
        for half in range(2):
            i = 2 * c + half
            ostage[i] = result[:, half * LANES : (half + 1) * LANES]
            device = member * heads + i
            dst = out.at[head_rows(head), :]
            copy = remote(ostage.at[i], dst, s_o.at[i], r_o.at[head], device)
            outs.append((copy, device))

            @pl.when(device == me)
            def _():
                pltpu.make_async_copy(ostage.at[i], dst, r_o.at[head]).start()

            @pl.when(device != me)
            def _():
                copy.start()

    attend(0)
    for d in range(1, group):
        landed(sinc.at[d - 1], r_sp.at[d - 1])
    total = sums[...]
    for d in range(1, group):
        total = total + sinc[d - 1]
    scale_send[0:4, :] = jnp.sqrt((total[0:4] + 1e-06) / (total[4:8] + 1e-06))
    scale_send[4:8, :] = total[4:8]
    for step in range(heads):
        i = lax.rem(head + step, heads)
        device = member + group * i
        if step == 0:
            pltpu.make_async_copy(gsend.at[i], g_out.at[head], r_g.at[head]).start()
            pltpu.make_async_copy(scale_send, scale_out.at[head], r_sc.at[head]).start()
        else:
            copy = remote(gsend.at[i], g_out.at[head], s_g.at[step], r_g.at[head], device)
            copy.start()
            pending.append(copy)
            copy = remote(scale_send, scale_out.at[head], s_sc.at[step], r_sc.at[head], device)
            copy.start()
            pending.append(copy)
    for c in range(1, span // chunk):
        attend(c)

    for i in range(heads):
        landed(g_out.at[i], r_g.at[i])
        landed(scale_out.at[i], r_sc.at[i])
        landed(out.at[pl.ds(i * width, width), :], r_o.at[i])
    for copy in pending:
        copy.wait_send()

    @pl.when(jnp.logical_not(is_self))
    def _():
        for copy in maybe:
            copy.wait_send()

    @pl.when(member < group - 1)
    def _():
        for copy in forwards:
            copy.wait_send()
    for copy, device in outs:
        @pl.when(device != me)
        def _():
            copy.wait_send()


def shards(queries, key_vectors, value_vectors, step_sizes, fast_weights, fast_gain, window_gain):
    tokens = queries.shape[0]
    heads = step_sizes.shape[1]
    width = queries.shape[1] // heads
    n = lax.axis_size("seq")
    group = n // heads
    rows = width // n
    assert tokens == LANES and heads * tokens == WINDOW
    head = lax.axis_index("seq") // group
    q_t, k_t, v_t = queries.T, key_vectors.T, value_vectors.T
    pieces = (
        fast_weights.astype(BF16).reshape(rows, 3, heads, width).transpose(2, 1, 0, 3)
        .reshape(heads, 3 * rows, width)
    )
    gains = jnp.stack([fast_gain.reshape(heads, width), window_gain.reshape(heads, width)], axis=1)
    gains = lax.dynamic_index_in_dim(gains, head, 0, keepdims=False)
    gains = jnp.broadcast_to(gains[:, :, None], (2, width, LANES))
    span = heads * LANES
    vmem = pl.BlockSpec(memory_space=pltpu.VMEM)
    dma = pltpu.SemaphoreType.DMA
    more = max(group - 1, 1)
    out_t, grads, scales = pl.pallas_call(
        functools.partial(kernel, n, heads, width),
        out_shape=(
            jax.ShapeDtypeStruct((heads * width, LANES), BF16),
            jax.ShapeDtypeStruct((heads, 3 * rows, width), BF16),
            jax.ShapeDtypeStruct((heads, 8, width), F32),
        ),
        in_specs=[vmem] * 6,
        out_specs=(vmem, vmem, vmem),
        scratch_shapes=[
            pltpu.VMEM((width, span), BF16),
            pltpu.VMEM((width, 2 * span), BF16),
            pltpu.VMEM((width, 2 * span), BF16),
            pltpu.VMEM((heads, heads, LANES), F32),
            pltpu.VMEM((n, 3 * rows, width), BF16),
            pltpu.VMEM((3, width, width), F32),
            pltpu.VMEM((2 * span, width), BF16),
            pltpu.VMEM((width, span), BF16),
            pltpu.VMEM((width, span), BF16),
            pltpu.VMEM((width, span), BF16),
            pltpu.VMEM((width, span), BF16),
            pltpu.VMEM((group, heads, 3 * rows, width), F32),
            pltpu.VMEM((more, heads, 3 * rows, width), F32),
            pltpu.VMEM((heads, 3 * rows, width), BF16),
            pltpu.VMEM((8, width), F32),
            pltpu.VMEM((more, 8, width), F32),
            pltpu.VMEM((8, width), F32),
            pltpu.VMEM((heads, width, LANES), BF16),
            dma((5, heads)), dma((heads,)), dma((2 * heads,)), dma((2 * heads,)), dma((heads,)), dma((n,)),
            dma((heads, more)), dma((heads,)), dma((heads,)),
            dma((more,)), dma((more,)), dma((more,)), dma((more,)),
            dma((heads,)), dma((heads,)), dma((heads,)), dma((heads,)), dma((heads,)), dma((heads,)),
        ],
        compiler_params=pltpu.CompilerParams(
            collective_id=0, has_side_effects=True, vmem_limit_bytes=60 << 20
        ),
        name="ttt",
    )(q_t, k_t, v_t, step_sizes.T, pieces, gains)
    layer_out = out_t.T
    momentum = (
        grads.astype(F32).reshape(heads, 3, rows, width).transpose(2, 1, 0, 3).reshape(rows, 3 * heads * width)
    )
    column_scale = scales[:, :3, :].transpose(1, 0, 2).reshape(1, -1)
    new_weights = (fast_weights - momentum) * column_scale
    return (layer_out, new_weights, momentum)


def solution(mesh):
    in_specs = (
        P(("groups", "seq"), None),
        P(("groups", "seq"), None),
        P(("groups", "seq"), None),
        P(("groups", "seq"), None),
        P("seq", None),
        P(),
        P(),
    )
    out_specs = (P(("groups", "seq"), None), P(("groups", "seq"), None), P(("groups", "seq"), None))
    return jax.shard_map(shards, mesh=mesh, in_specs=in_specs, out_specs=out_specs, check_vma=False)
```

```python
import functools
import math

import jax
import jax.numpy as jnp
from jax import lax
from jax.experimental import pallas as pl
from jax.experimental.pallas import tpu as pltpu
from jax.sharding import PartitionSpec as P

WINDOW = 1024
LANES = 128
F32 = jnp.float32
BF16 = jnp.bfloat16


def dot(a, b):
    return jnp.dot(a, b, preferred_element_type=F32)


def dot_nt(a, b):
    return lax.dot_general(a, b, (((1,), (1,)), ((), ())), preferred_element_type=F32)


def dot_tn(a, b):
    return lax.dot_general(a, b, (((0,), (0,)), ((), ())), preferred_element_type=F32)


def kernel(
    n, groups, heads, width,
    q_in, k_in, v_in, step_in, w_in, gains,
    out, g_out, scale_out,
    qb, kb, vb, stb, wb, wfull, kn, hid, tgt, gg, gu,
    gstage, ginc, gsend, sums, sinc, scale_send, ostage,
    s_in, r_q, r_k, r_v, r_st, r_w,
    s_wf, s_kf, s_vf,
    s_gp, r_gp, s_sp, r_sp, s_g, r_g, s_sc, r_sc, s_o, r_o,
):
    group = n // heads
    rows = width // n
    span = heads * LANES
    scale = 1.0 / math.sqrt(width)
    me = lax.axis_index("seq")
    part = lax.axis_index("groups")
    head = me // group
    member = me % group
    block_member = me // heads
    block_slot = me % heads

    def remote(src, dst, send, recv, device, to_part=None):
        return pltpu.make_async_remote_copy(
            src_ref=src, dst_ref=dst, send_sem=send, recv_sem=recv,
            device_id={"groups": part if to_part is None else to_part, "seq": device},
            device_id_type=pl.DeviceIdType.MESH,
        )

    barrier = pltpu.get_barrier_semaphore()
    for step in range(1, n):
        pl.semaphore_signal(
            barrier, inc=1, device_id={"seq": lax.rem(me + step, n)},
            device_id_type=pl.DeviceIdType.MESH,
        )
    for other in range(1, groups):
        for d in range(group):
            pl.semaphore_signal(
                barrier, inc=1,
                device_id={"groups": lax.rem(part + other, groups), "seq": head * group + d},
                device_id_type=pl.DeviceIdType.MESH,
            )
    pl.semaphore_wait(barrier, n - 1 + (groups - 1) * group)

    def head_rows(which):
        return pl.ds(pl.multiple_of(which * width, 64), width)

    is_self = block_member == member
    pending = []
    maybe = []

    def spread(src_of, dst, recv, kind):
        for step in range(heads):
            which = lax.rem(head + step, heads)
            device = which * group + block_member
            src = src_of(which)
            copy = remote(src, dst, s_in.at[kind, step], recv, device)
            if step == 0:
                @pl.when(is_self)
                def _():
                    pltpu.make_async_copy(src, dst, recv).start()

                @pl.when(jnp.logical_not(is_self))
                def _():
                    copy.start()
                maybe.append(copy)
            else:
                copy.start()
                pending.append(copy)

    stride = heads // groups
    shift = lax.rem(part + groups * heads - 2 * head, groups)
    w_maybe = []
    for step in range(stride):
        offset = shift + groups * step
        which = lax.rem(head + offset, heads)
        copy = remote(w_in.at[which], wb.at[me], s_in.at[4, step], r_w.at[me], which * group + member)
        if step == 0:
            @pl.when(offset == 0)
            def _():
                pltpu.make_async_copy(w_in.at[which], wb.at[me], r_w.at[me]).start()

            @pl.when(offset != 0)
            def _():
                copy.start()
            w_maybe.append(copy)
        else:
            copy.start()
            pending.append(copy)
    own = heads + block_slot
    spread(lambda w: k_in.at[head_rows(w), :], kb.at[own], r_k.at[own], 0)
    spread(lambda w: v_in.at[head_rows(w), :], vb.at[own], r_v.at[own], 1)
    spread(lambda w: step_in, stb.at[block_slot], r_st.at[block_slot], 2)
    spread(lambda w: q_in.at[head_rows(w), :], qb.at[block_slot], r_q.at[block_slot], 3)

    @pl.when(member == 0)
    def _():
        kb[:heads] = jnp.zeros((heads, width, LANES), BF16)
        vb[:heads] = jnp.zeros((heads, width, LANES), BF16)

    def landed(ref, sem):
        pltpu.make_async_copy(ref, ref, sem).wait()

    first = lax.rem(part + groups * heads - head, groups)
    for t in range(stride):
        slot = member + group * (first + groups * t)
        landed(wb.at[slot], r_w.at[slot])
        for other in range(groups):
            for d in range(group):
                if other + d == 0:
                    continue
                copy = remote(
                    wb.at[slot], wb.at[slot], s_wf.at[t, other * group + d], r_w.at[slot],
                    head * group + lax.rem(member + d, group), lax.rem(part + other, groups),
                )
                copy.start()
                pending.append(copy)

    forwards = []
    for i in range(heads):
        for buf, send, recv in ((kb, s_kf, r_k), (vb, s_vf, r_v)):
            landed(buf.at[heads + i], recv.at[heads + i])
            copy = remote(buf.at[heads + i], buf.at[i], send.at[i], recv.at[i], me + 1)
            forwards.append(copy)

            @pl.when(member < group - 1)
            def _():
                copy.start()
    for d in range(group):
        for e in range(groups):
            if d + e == 0:
                continue
            for t in range(stride):
                slot = lax.rem(member + d, group) + group * (lax.rem(first + e, groups) + groups * t)
                landed(wb.at[slot], r_w.at[slot])
    for s in range(n):
        piece = wb[s].astype(F32)
        for m in range(3):
            wfull[m, s * rows : (s + 1) * rows, :] = piece[m * rows : (m + 1) * rows, :]
    for i in range(heads):
        landed(stb.at[i], r_st.at[i])

    w1 = wfull[0].astype(BF16)
    w3 = wfull[1].astype(BF16)
    w2 = wfull[2].astype(BF16)

    for i in range(heads):
        there = pl.ds(i * LANES, LANES)
        tgt[:, there] = (-stb[i, pl.ds(head, 1), :] * vb[heads + i].astype(F32)).astype(BF16)
    chunk = 2 * LANES

    def grad_chunk(c, carry):
        there = pl.ds(pl.multiple_of(c * chunk, chunk), chunk)
        keys = jnp.concatenate([kb[heads + 2 * c], kb[heads + 2 * c + 1]], axis=1)
        gate = dot_tn(w1, keys) * scale
        up = dot_tn(w3, keys) * scale
        back = dot(w2, tgt[:, there]) * scale
        sigma = jax.nn.sigmoid(gate)
        silu = gate * sigma
        hid[:, there] = (silu * up).astype(BF16)
        gg[:, there] = (back * up * (sigma * (1.0 + gate * (1.0 - sigma)))).astype(BF16)
        gu[:, there] = (back * silu).astype(BF16)
        return carry

    lax.fori_loop(0, span // chunk, grad_chunk, 0)
    own_keys = jnp.concatenate([kb[heads + i] for i in range(heads)], axis=1)
    for m, (left, right) in enumerate(((own_keys, gg), (own_keys, gu), (hid[...], tgt))):
        grad = dot_nt(left, right[...]) * scale
        for s in range(n):
            gstage[s % group, s // group, m * rows : (m + 1) * rows, :] = grad[s * rows : (s + 1) * rows, :]

    for d in range(1, group):
        other = lax.rem(member + d, group)
        copy = remote(
            gstage.at[other], ginc.at[d - 1], s_gp.at[d - 1], r_gp.at[d - 1], head * group + other
        )
        copy.start()
        pending.append(copy)

    @pl.when(member > 0)
    def _():
        for i in range(heads):
            landed(kb.at[i], r_k.at[i])
            landed(vb.at[i], r_v.at[i])

    def flip(c, carry):
        at = pl.ds(pl.multiple_of(c * LANES, LANES), LANES)
        kn[at, :] = kb[c].T
        return carry

    lax.fori_loop(0, 2 * heads, flip, 0)

    for d in range(1, group):
        landed(ginc.at[d - 1], r_gp.at[d - 1])
    sums[...] = jnp.zeros_like(sums)

    def add_up(i, carry):
        total = gstage[member, i]
        for d in range(1, group):
            total = total + ginc[d - 1, i]
        gsend[i] = total.astype(BF16)
        weight = wb[member + group * i].astype(F32)
        moved = weight - total
        for m in range(3):
            part = slice(m * rows, (m + 1) * rows)
            old = weight[part, :]
            new = moved[part, :]
            sums[m : m + 1, :] += jnp.sum(old * old, axis=0, keepdims=True)
            sums[4 + m : 5 + m, :] += jnp.sum(new * new, axis=0, keepdims=True)
        return carry

    lax.fori_loop(0, heads, add_up, 0)
    for d in range(1, group):
        copy = remote(
            sums, sinc.at[d - 1], s_sp.at[d - 1], r_sp.at[d - 1],
            head * group + lax.rem(member + d, group),
        )
        copy.start()
        pending.append(copy)

    for i in range(heads):
        landed(qb.at[i], r_q.at[i])

    reach = WINDOW + chunk
    key_at = lax.broadcasted_iota(jnp.int32, (reach, chunk), 0)
    query_at = lax.broadcasted_iota(jnp.int32, (reach, chunk), 1)
    distance = WINDOW + query_at - key_at
    in_window = (distance >= 0) & (distance < WINDOW)
    first_key = jnp.where(member == 0, span, 0)

    def normalize(field, gain):
        mean_sq = jnp.mean(field * field, axis=0, keepdims=True)
        return field * lax.rsqrt(mean_sq + 1e-05) * gain

    outs = []

    def attend(c):
        start = c * chunk
        query = jnp.concatenate([qb[2 * c], qb[2 * c + 1]], axis=1)
        scores = dot(kn[pl.ds(start, reach), :], query) * scale
        allowed = in_window & (key_at + start >= first_key)
        scores = jnp.where(allowed, scores, -1e30)
        weights = jnp.exp(scores - jnp.max(scores, axis=0, keepdims=True))
        probs = (weights / jnp.sum(weights, axis=0, keepdims=True)).astype(BF16)
        values = jnp.concatenate([vb[2 * c + i] for i in range(reach // LANES)], axis=1)
        attended = dot(values, probs)
        window_part = normalize(attended, gains[1, :, 0:1])
        gate = dot_tn(w1, query) * scale
        up = dot_tn(w3, query) * scale
        hidden = (gate * jax.nn.sigmoid(gate) * up).astype(BF16)
        fast_part = normalize(dot_tn(w2, hidden) * scale, gains[0, :, 0:1])
        result = (fast_part + window_part).astype(BF16)
        for half in range(2):
            i = 2 * c + half
            ostage[i] = result[:, half * LANES : (half + 1) * LANES]
            device = member * heads + i
            dst = out.at[head_rows(head), :]
            copy = remote(ostage.at[i], dst, s_o.at[i], r_o.at[head], device)
            outs.append((copy, device))

            @pl.when(device == me)
            def _():
                pltpu.make_async_copy(ostage.at[i], dst, r_o.at[head]).start()

            @pl.when(device != me)
            def _():
                copy.start()

    attend(0)
    for d in range(1, group):
        landed(sinc.at[d - 1], r_sp.at[d - 1])
    total = sums[...]
    for d in range(1, group):
        total = total + sinc[d - 1]
    scale_send[0:4, :] = jnp.sqrt((total[0:4] + 1e-06) / (total[4:8] + 1e-06))
    scale_send[4:8, :] = total[4:8]
    for step in range(heads):
        i = lax.rem(head + step, heads)
        device = member + group * i
        if step == 0:
            pltpu.make_async_copy(gsend.at[i], g_out.at[head], r_g.at[head]).start()
            pltpu.make_async_copy(scale_send, scale_out.at[head], r_sc.at[head]).start()
        else:
            copy = remote(gsend.at[i], g_out.at[head], s_g.at[step], r_g.at[head], device)
            copy.start()
            pending.append(copy)
            copy = remote(scale_send, scale_out.at[head], s_sc.at[step], r_sc.at[head], device)
            copy.start()
            pending.append(copy)
    for c in range(1, span // chunk):
        attend(c)

    for i in range(heads):
        landed(g_out.at[i], r_g.at[i])
        landed(scale_out.at[i], r_sc.at[i])
        landed(out.at[pl.ds(i * width, width), :], r_o.at[i])
    for copy in pending:
        copy.wait_send()

    @pl.when(jnp.logical_not(is_self))
    def _():
        for copy in maybe:
            copy.wait_send()

    @pl.when(shift != 0)
    def _():
        for copy in w_maybe:
            copy.wait_send()

    @pl.when(member < group - 1)
    def _():
        for copy in forwards:
            copy.wait_send()
    for copy, device in outs:
        @pl.when(device != me)
        def _():
            copy.wait_send()


def shards(queries, key_vectors, value_vectors, step_sizes, fast_weights, fast_gain, window_gain):
    tokens = queries.shape[0]
    heads = step_sizes.shape[1]
    width = queries.shape[1] // heads
    n = lax.axis_size("seq")
    groups = lax.axis_size("groups")
    group = n // heads
    rows = width // n
    assert tokens == LANES and heads * tokens == WINDOW
    head = lax.axis_index("seq") // group
    q_t, k_t, v_t = queries.T, key_vectors.T, value_vectors.T
    pieces = (
        fast_weights.astype(BF16).reshape(rows, 3, heads, width).transpose(2, 1, 0, 3)
        .reshape(heads, 3 * rows, width)
    )
    gains = jnp.stack([fast_gain.reshape(heads, width), window_gain.reshape(heads, width)], axis=1)
    gains = lax.dynamic_index_in_dim(gains, head, 0, keepdims=False)
    gains = jnp.broadcast_to(gains[:, :, None], (2, width, LANES))
    span = heads * LANES
    vmem = pl.BlockSpec(memory_space=pltpu.VMEM)
    dma = pltpu.SemaphoreType.DMA
    more = max(group - 1, 1)
    out_t, grads, scales = pl.pallas_call(
        functools.partial(kernel, n, groups, heads, width),
        out_shape=(
            jax.ShapeDtypeStruct((heads * width, LANES), BF16),
            jax.ShapeDtypeStruct((heads, 3 * rows, width), BF16),
            jax.ShapeDtypeStruct((heads, 8, width), F32),
        ),
        in_specs=[vmem] * 6,
        out_specs=(vmem, vmem, vmem),
        scratch_shapes=[
            pltpu.VMEM((heads, width, LANES), BF16),
            pltpu.VMEM((2 * heads, width, LANES), BF16),
            pltpu.VMEM((2 * heads, width, LANES), BF16),
            pltpu.VMEM((heads, heads, LANES), F32),
            pltpu.VMEM((n, 3 * rows, width), BF16),
            pltpu.VMEM((3, width, width), F32),
            pltpu.VMEM((2 * span, width), BF16),
            pltpu.VMEM((width, span), BF16),
            pltpu.VMEM((width, span), BF16),
            pltpu.VMEM((width, span), BF16),
            pltpu.VMEM((width, span), BF16),
            pltpu.VMEM((group, heads, 3 * rows, width), F32),
            pltpu.VMEM((more, heads, 3 * rows, width), F32),
            pltpu.VMEM((heads, 3 * rows, width), BF16),
            pltpu.VMEM((8, width), F32),
            pltpu.VMEM((more, 8, width), F32),
            pltpu.VMEM((8, width), F32),
            pltpu.VMEM((heads, width, LANES), BF16),
            dma((5, heads)), dma((heads,)), dma((2 * heads,)), dma((2 * heads,)), dma((heads,)), dma((n,)),
            dma((heads // groups, groups * group)), dma((heads,)), dma((heads,)),
            dma((more,)), dma((more,)), dma((more,)), dma((more,)),
            dma((heads,)), dma((heads,)), dma((heads,)), dma((heads,)), dma((heads,)), dma((heads,)),
        ],
        compiler_params=pltpu.CompilerParams(
            collective_id=0, has_side_effects=True, vmem_limit_bytes=60 << 20
        ),
        name="ttt",
    )(q_t, k_t, v_t, step_sizes.T, pieces, gains)
    layer_out = out_t.T
    momentum = (
        grads.astype(F32).reshape(heads, 3, rows, width).transpose(2, 1, 0, 3).reshape(rows, 3 * heads * width)
    )
    column_scale = scales[:, :3, :].transpose(1, 0, 2).reshape(1, -1)
    new_weights = (fast_weights - momentum) * column_scale
    return (layer_out, new_weights, momentum)


def solution(mesh):
    in_specs = (
        P(("groups", "seq"), None),
        P(("groups", "seq"), None),
        P(("groups", "seq"), None),
        P(("groups", "seq"), None),
        P("seq", None),
        P(),
        P(),
    )
    out_specs = (P(("groups", "seq"), None), P(("groups", "seq"), None), P(("groups", "seq"), None))
    return jax.shard_map(shards, mesh=mesh, in_specs=in_specs, out_specs=out_specs, check_vma=False)
```

```python
import functools
import math

import jax
import jax.numpy as jnp
from jax import lax
from jax.experimental import pallas as pl
from jax.experimental.pallas import tpu as pltpu
from jax.sharding import PartitionSpec as P

WINDOW = 1024
LANES = 128
F32 = jnp.float32
BF16 = jnp.bfloat16


def dot(a, b):
    return jnp.dot(a, b, preferred_element_type=F32)


def dot_nt(a, b):
    return lax.dot_general(a, b, (((1,), (1,)), ((), ())), preferred_element_type=F32)


def dot_tn(a, b):
    return lax.dot_general(a, b, (((0,), (0,)), ((), ())), preferred_element_type=F32)


def kernel(
    n, groups, heads, width,
    kvq_in, step_in, w_in, fast_gain, window_gain,
    out, g_out, scale_out,
    kv, qb, stb, wb, wfull, kn, hid, tgt, gg, gu,
    gstage, ginc, gsend, sums, sinc, scale_send, ostage,
    s_in, r_k, r_v, r_q, r_prior, r_st, r_w,
    s_wf, s_kf,
    s_gp, r_gp, s_sp, r_sp, s_g, r_g, s_sc, r_sc, s_o, r_o,
):
    group = n // heads
    rows = width // n
    span = heads * LANES
    scale = 1.0 / math.sqrt(width)
    me = lax.axis_index("seq")
    part = lax.axis_index("groups")
    head = me // group
    member = me % group
    block_member = me // heads
    block_slot = me % heads

    def remote(src, dst, send, recv, device, to_part=None):
        return pltpu.make_async_remote_copy(
            src_ref=src, dst_ref=dst, send_sem=send, recv_sem=recv,
            device_id={"groups": part if to_part is None else to_part, "seq": device},
            device_id_type=pl.DeviceIdType.MESH,
        )

    barrier = pltpu.get_barrier_semaphore()
    for step in range(1, n):
        pl.semaphore_signal(
            barrier, inc=1, device_id={"seq": lax.rem(me + step, n)},
            device_id_type=pl.DeviceIdType.MESH,
        )
    for other in range(1, groups):
        for d in range(group):
            pl.semaphore_signal(
                barrier, inc=1,
                device_id={"groups": lax.rem(part + other, groups), "seq": head * group + d},
                device_id_type=pl.DeviceIdType.MESH,
            )
    pl.semaphore_wait(barrier, n - 1 + (groups - 1) * group)

    def head_rows(which):
        return pl.ds(pl.multiple_of(which * width, 64), width)

    is_self = block_member == member
    pending = []
    maybe = []

    def flip_bits(value, bits):
        for bit in (1, 2, 4):
            if bits & bit:
                value = value + bit - 2 * bit * lax.rem(value // bit, 2)
        return value

    order = range(heads)

    def spread(src_of, dst, recv, kind):
        for step in order:
            which = lax.rem(head + step, heads)
            device = which * group + block_member
            src = src_of(which)
            copy = remote(src, dst, s_in.at[kind, step], recv, device)
            if step == 0:
                @pl.when(is_self)
                def _():
                    pltpu.make_async_copy(src, dst, recv).start()

                @pl.when(jnp.logical_not(is_self))
                def _():
                    copy.start()
                maybe.append(copy)
            else:
                copy.start()
                pending.append(copy)

    stride = heads // groups
    shift = lax.rem(part + groups * heads - 2 * head, groups)
    w_maybe = []
    for step in range(stride):
        offset = shift + groups * step
        which = lax.rem(head + offset, heads)
        copy = remote(w_in.at[which], wb.at[me], s_in.at[4, step], r_w.at[me], which * group + member)
        if step == 0:
            @pl.when(offset == 0)
            def _():
                pltpu.make_async_copy(w_in.at[which], wb.at[me], r_w.at[me]).start()

            @pl.when(offset != 0)
            def _():
                copy.start()
            w_maybe.append(copy)
        else:
            copy.start()
            pending.append(copy)
    spread(lambda w: kvq_in.at[w, 0], kv.at[heads + block_slot, 0], r_k.at[block_slot], 0)
    spread(lambda w: kvq_in.at[w, 1], kv.at[heads + block_slot, 1], r_v.at[block_slot], 1)
    spread(lambda w: step_in, stb.at[block_slot], r_st.at[block_slot], 2)
    spread(lambda w: kvq_in.at[w, 2], qb.at[block_slot], r_q.at[block_slot], 3)

    @pl.when(member == 0)
    def _():
        kv[:heads] = jnp.zeros((heads, 2, width, LANES), BF16)

    def landed(ref, sem):
        pltpu.make_async_copy(ref, ref, sem).wait()

    first = lax.rem(part + groups * heads - head, groups)
    for t in range(stride):
        slot = member + group * (first + groups * t)
        landed(wb.at[slot], r_w.at[slot])
        for other in range(groups):
            for d in range(group):
                if other + d == 0:
                    continue
                copy = remote(
                    wb.at[slot], wb.at[slot], s_wf.at[t, other * group + d], r_w.at[slot],
                    head * group + lax.rem(member + d, group), lax.rem(part + other, groups),
                )
                copy.start()
                pending.append(copy)

    forwards = []
    for i in range(heads):
        landed(kv.at[heads + i, 0], r_k.at[i])
        landed(kv.at[heads + i, 1], r_v.at[i])
        copy = remote(kv.at[heads + i], kv.at[i], s_kf.at[i], r_prior.at[i], me + 1)
        forwards.append(copy)

        @pl.when(member < group - 1)
        def _():
            copy.start()
    for d in range(group):
        for e in range(groups):
            if d + e == 0:
                continue
            for t in range(stride):
                slot = lax.rem(member + d, group) + group * (lax.rem(first + e, groups) + groups * t)
                landed(wb.at[slot], r_w.at[slot])
    for s in range(n):
        piece = wb[s].astype(F32)
        for m in range(3):
            wfull[m, s * rows : (s + 1) * rows, :] = piece[m * rows : (m + 1) * rows, :]
    for i in range(heads):
        landed(stb.at[i], r_st.at[i])

    w1 = wfull[0].astype(BF16)
    w3 = wfull[1].astype(BF16)
    w2 = wfull[2].astype(BF16)

    for i in range(heads):
        there = pl.ds(i * LANES, LANES)
        tgt[:, there] = (-stb[i, pl.ds(head, 1), :] * kv[heads + i, 1].astype(F32)).astype(BF16)
    chunk = 2 * LANES

    def grad_chunk(c, carry):
        there = pl.ds(pl.multiple_of(c * chunk, chunk), chunk)
        keys = jnp.concatenate([kv[heads + 2 * c, 0], kv[heads + 2 * c + 1, 0]], axis=1)
        gate = dot_tn(w1, keys) * scale
        up = dot_tn(w3, keys) * scale
        back = dot(w2, tgt[:, there]) * scale
        sigma = jax.nn.sigmoid(gate)
        silu = gate * sigma
        hid[:, there] = (silu * up).astype(BF16)
        gg[:, there] = (back * up * (sigma * (1.0 + gate * (1.0 - sigma)))).astype(BF16)
        gu[:, there] = (back * silu).astype(BF16)
        return carry

    lax.fori_loop(0, span // chunk, grad_chunk, 0)
    own_keys = jnp.concatenate([kv[heads + i, 0] for i in range(heads)], axis=1)
    for m, (left, right) in enumerate(((own_keys, gg), (own_keys, gu), (hid[...], tgt))):
        grad = dot_nt(left, right[...]) * scale
        for s in range(n):
            gstage[s % group, s // group, m * rows : (m + 1) * rows, :] = grad[s * rows : (s + 1) * rows, :]

    for d in range(1, group):
        other = lax.rem(member + d, group)
        copy = remote(
            gstage.at[other], ginc.at[d - 1], s_gp.at[d - 1], r_gp.at[d - 1], head * group + other
        )
        copy.start()
        pending.append(copy)

    @pl.when(member > 0)
    def _():
        for i in range(heads):
            landed(kv.at[i], r_prior.at[i])

    def flip(c, carry):
        at = pl.ds(pl.multiple_of(c * LANES, LANES), LANES)
        kn[at, :] = kv[c, 0].T
        return carry

    lax.fori_loop(0, 2 * heads, flip, 0)

    for d in range(1, group):
        landed(ginc.at[d - 1], r_gp.at[d - 1])
    sums[...] = jnp.zeros_like(sums)

    def add_up(i, carry):
        total = gstage[member, i]
        for d in range(1, group):
            total = total + ginc[d - 1, i]
        gsend[i] = total.astype(BF16)
        weight = wb[member + group * i].astype(F32)
        moved = weight - total
        for m in range(3):
            part = slice(m * rows, (m + 1) * rows)
            old = weight[part, :]
            new = moved[part, :]
            sums[m : m + 1, :] += jnp.sum(old * old, axis=0, keepdims=True)
            sums[4 + m : 5 + m, :] += jnp.sum(new * new, axis=0, keepdims=True)
        return carry

    lax.fori_loop(0, heads, add_up, 0)
    for d in range(1, group):
        copy = remote(
            sums, sinc.at[d - 1], s_sp.at[d - 1], r_sp.at[d - 1],
            head * group + lax.rem(member + d, group),
        )
        copy.start()
        pending.append(copy)


    for i in range(heads):
        landed(qb.at[i], r_q.at[i])

    reach = WINDOW + chunk
    key_at = lax.broadcasted_iota(jnp.int32, (reach, chunk), 0)
    query_at = lax.broadcasted_iota(jnp.int32, (reach, chunk), 1)
    distance = WINDOW + query_at - key_at
    in_window = (distance >= 0) & (distance < WINDOW)
    first_key = jnp.where(member == 0, span, 0)

    def gain_column(ref):
        return jnp.broadcast_to(ref[pl.ds(head, 1), :], (8, width)).T[:, 0:1]

    fast_column = gain_column(fast_gain)
    window_column = gain_column(window_gain)

    def normalize(field, gain):
        mean_sq = jnp.mean(field * field, axis=0, keepdims=True)
        return field * lax.rsqrt(mean_sq + 1e-05) * gain

    outs = []

    def attend(turn):
        c = turn
        start = c * chunk
        query = jnp.concatenate([qb[2 * c], qb[2 * c + 1]], axis=1)
        scores = dot(kn[pl.ds(start, reach), :], query) * scale
        allowed = in_window & (key_at + start >= first_key)
        scores = jnp.where(allowed, scores, -1e30)
        weights = jnp.exp(scores - jnp.max(scores, axis=0, keepdims=True))
        probs = (weights / jnp.sum(weights, axis=0, keepdims=True)).astype(BF16)
        values = jnp.concatenate([kv[2 * c + i, 1] for i in range(reach // LANES)], axis=1)
        attended = dot(values, probs)
        window_part = normalize(attended, window_column)
        gate = dot_tn(w1, query) * scale
        up = dot_tn(w3, query) * scale
        hidden = (gate * jax.nn.sigmoid(gate) * up).astype(BF16)
        fast_part = normalize(dot_tn(w2, hidden) * scale, fast_column)
        result = (fast_part + window_part).astype(BF16)
        for half in range(2):
            i = 2 * c + half
            ostage[i] = result[:, half * LANES : (half + 1) * LANES]
            device = member * heads + i
            dst = out.at[head_rows(head), :]
            copy = remote(ostage.at[i], dst, s_o.at[i], r_o.at[head], device)
            outs.append((copy, device))

            @pl.when(device == me)
            def _():
                pltpu.make_async_copy(ostage.at[i], dst, r_o.at[head]).start()

            @pl.when(device != me)
            def _():
                copy.start()

    attend(0)
    for d in range(1, group):
        landed(sinc.at[d - 1], r_sp.at[d - 1])
    total = sums[...]
    for d in range(1, group):
        total = total + sinc[d - 1]
    scale_send[0:4, :] = jnp.sqrt((total[0:4] + 1e-06) / (total[4:8] + 1e-06))
    scale_send[4:8, :] = total[4:8]
    for step in range(heads):
        i = lax.rem(head + step, heads)
        device = member + group * i
        if step == 0:
            pltpu.make_async_copy(gsend.at[i], g_out.at[head], r_g.at[head]).start()
            pltpu.make_async_copy(scale_send, scale_out.at[head], r_sc.at[head]).start()
        else:
            copy = remote(gsend.at[i], g_out.at[head], s_g.at[step], r_g.at[head], device)
            copy.start()
            pending.append(copy)
            copy = remote(scale_send, scale_out.at[head], s_sc.at[step], r_sc.at[head], device)
            copy.start()
            pending.append(copy)
    for c in range(1, span // chunk):
        attend(c)

    for i in range(heads):
        landed(g_out.at[i], r_g.at[i])
        landed(scale_out.at[i], r_sc.at[i])
        landed(out.at[pl.ds(i * width, width), :], r_o.at[i])
    for copy in pending:
        copy.wait_send()

    @pl.when(jnp.logical_not(is_self))
    def _():
        for copy in maybe:
            copy.wait_send()

    @pl.when(shift != 0)
    def _():
        for copy in w_maybe:
            copy.wait_send()

    @pl.when(member < group - 1)
    def _():
        for copy in forwards:
            copy.wait_send()
    for copy, device in outs:
        @pl.when(device != me)
        def _():
            copy.wait_send()


def prepare(heads, width, rows, k, v, q, weights, kvq, pieces, wide):
    for m, ref in enumerate((k, v, q)):
        flipped = ref[...].T
        for h in range(heads):
            kvq[h, m] = flipped[h * width : (h + 1) * width]
    for h in range(heads):
        for m in range(3):
            at = (m * heads + h) * width
            wide[h, m * rows : (m + 1) * rows, :] = weights[:, at : at + width]
        pieces[h] = wide[h].astype(BF16)


def finish(heads, width, rows, out_t, grads, scales, weights, layer_out, new_weights, momentum):
    layer_out[...] = out_t[...].T
    for h in range(heads):
        grad = grads[h].astype(F32)
        for m in range(3):
            at = (m * heads + h) * width
            part = grad[m * rows : (m + 1) * rows, :]
            momentum[:, at : at + width] = part
            new_weights[:, at : at + width] = (weights[:, at : at + width] - part) * scales[h, m : m + 1, :]


def shards(queries, key_vectors, value_vectors, step_sizes, fast_weights, fast_gain, window_gain):
    tokens = queries.shape[0]
    heads = step_sizes.shape[1]
    width = queries.shape[1] // heads
    n = lax.axis_size("seq")
    groups = lax.axis_size("groups")
    group = n // heads
    rows = width // n
    assert tokens == LANES and heads * tokens == WINDOW
    span = heads * LANES
    vmem = pl.BlockSpec(memory_space=pltpu.VMEM)
    dma = pltpu.SemaphoreType.DMA
    more = max(group - 1, 1)
    kvq, pieces = pl.pallas_call(
        functools.partial(prepare, heads, width, rows),
        out_shape=(
            jax.ShapeDtypeStruct((heads, 3, width, LANES), BF16),
            jax.ShapeDtypeStruct((heads, 3 * rows, width), BF16),
        ),
        in_specs=[vmem] * 4,
        out_specs=(vmem, vmem),
        scratch_shapes=[pltpu.VMEM((heads, 3 * rows, width), F32)],
        name="prepare",
    )(key_vectors, value_vectors, queries, fast_weights)
    out_t, grads, scales = pl.pallas_call(
        functools.partial(kernel, n, groups, heads, width),
        out_shape=(
            jax.ShapeDtypeStruct((heads * width, LANES), BF16),
            jax.ShapeDtypeStruct((heads, 3 * rows, width), BF16),
            jax.ShapeDtypeStruct((heads, 8, width), F32),
        ),
        in_specs=[vmem] * 5,
        out_specs=(vmem, vmem, vmem),
        scratch_shapes=[
            pltpu.VMEM((2 * heads, 2, width, LANES), BF16),
            pltpu.VMEM((heads, width, LANES), BF16),
            pltpu.VMEM((heads, heads, LANES), F32),
            pltpu.VMEM((n, 3 * rows, width), BF16),
            pltpu.VMEM((3, width, width), F32),
            pltpu.VMEM((2 * span, width), BF16),
            pltpu.VMEM((width, span), BF16),
            pltpu.VMEM((width, span), BF16),
            pltpu.VMEM((width, span), BF16),
            pltpu.VMEM((width, span), BF16),
            pltpu.VMEM((group, heads, 3 * rows, width), F32),
            pltpu.VMEM((more, heads, 3 * rows, width), F32),
            pltpu.VMEM((heads, 3 * rows, width), BF16),
            pltpu.VMEM((8, width), F32),
            pltpu.VMEM((more, 8, width), F32),
            pltpu.VMEM((8, width), F32),
            pltpu.VMEM((heads, width, LANES), BF16),
            dma((5, heads)), dma((heads,)), dma((heads,)), dma((heads,)), dma((heads,)), dma((heads,)), dma((n,)),
            dma((heads // groups, groups * group)), dma((heads,)),
            dma((more,)), dma((more,)), dma((more,)), dma((more,)),
            dma((heads,)), dma((heads,)), dma((heads,)), dma((heads,)), dma((heads,)), dma((heads,)),
        ],
        compiler_params=pltpu.CompilerParams(
            collective_id=0, has_side_effects=True, vmem_limit_bytes=60 << 20
        ),
        name="ttt",
    )(kvq, step_sizes.T, pieces, fast_gain.reshape(heads, width), window_gain.reshape(heads, width))
    return pl.pallas_call(
        functools.partial(finish, heads, width, rows),
        out_shape=(
            jax.ShapeDtypeStruct(queries.shape, BF16),
            jax.ShapeDtypeStruct(fast_weights.shape, F32),
            jax.ShapeDtypeStruct(fast_weights.shape, F32),
        ),
        in_specs=[vmem] * 4,
        out_specs=(vmem, vmem, vmem),
        name="finish",
    )(out_t, grads, scales, fast_weights)


def solution(mesh):
    in_specs = (
        P(("groups", "seq"), None),
        P(("groups", "seq"), None),
        P(("groups", "seq"), None),
        P(("groups", "seq"), None),
        P("seq", None),
        P(),
        P(),
    )
    out_specs = (P(("groups", "seq"), None), P(("groups", "seq"), None), P(("groups", "seq"), None))
    return jax.shard_map(shards, mesh=mesh, in_specs=in_specs, out_specs=out_specs, check_vma=False)
```

```python
import functools
import math

import jax
import jax.numpy as jnp
from jax import lax
from jax.experimental import pallas as pl
from jax.experimental.pallas import tpu as pltpu
from jax.sharding import PartitionSpec as P

WINDOW = 1024
LANES = 128
F32 = jnp.float32
BF16 = jnp.bfloat16


def dot(a, b):
    return jnp.dot(a, b, preferred_element_type=F32)


def dot_nt(a, b):
    return lax.dot_general(a, b, (((1,), (1,)), ((), ())), preferred_element_type=F32)


def dot_tn(a, b):
    return lax.dot_general(a, b, (((0,), (0,)), ((), ())), preferred_element_type=F32)


def kernel(
    n, groups, heads, width,
    kvq_in, step_in, w_in, fast_gain, window_gain,
    out, g_out, scale_out,
    kv, qb, stb, wb, wfull, kn, hid, tgt, gg, gu,
    gstage, ginc, gsend, sums, sinc, scale_send, ostage, gain_rows,
    s_in, r_k, r_v, r_q, r_prior, r_st, r_w,
    s_wf, s_kf,
    s_gp, r_gp, s_sp, r_sp, s_g, r_g, s_sc, r_sc, s_o, r_o,
):
    group = n // heads
    rows = width // n
    span = heads * LANES
    scale = 1.0 / math.sqrt(width)
    me = lax.axis_index("seq")
    part = lax.axis_index("groups")
    head = me // group
    member = me % group
    block_member = me // heads
    block_slot = me % heads

    def remote(src, dst, send, recv, device, to_part=None):
        return pltpu.make_async_remote_copy(
            src_ref=src, dst_ref=dst, send_sem=send, recv_sem=recv,
            device_id={"groups": part if to_part is None else to_part, "seq": device},
            device_id_type=pl.DeviceIdType.MESH,
        )

    barrier = pltpu.get_barrier_semaphore()
    for step in range(1, n):
        pl.semaphore_signal(
            barrier, inc=1, device_id={"seq": lax.rem(me + step, n)},
            device_id_type=pl.DeviceIdType.MESH,
        )
    for other in range(1, groups):
        for d in range(group):
            pl.semaphore_signal(
                barrier, inc=1,
                device_id={"groups": lax.rem(part + other, groups), "seq": head * group + d},
                device_id_type=pl.DeviceIdType.MESH,
            )
    pl.semaphore_wait(barrier, n - 1 + (groups - 1) * group)

    def head_rows(which):
        return pl.ds(pl.multiple_of(which * width, 64), width)

    is_self = block_member == member
    pending = []
    maybe = []

    def flip_bits(value, bits):
        for bit in (1, 2, 4):
            if bits & bit:
                value = value + bit - 2 * bit * lax.rem(value // bit, 2)
        return value

    order = range(heads)

    def spread(src_of, dst, recv, kind):
        for step in order:
            which = lax.rem(head + step, heads)
            device = which * group + block_member
            src = src_of(which)
            copy = remote(src, dst, s_in.at[kind, step], recv, device)
            if step == 0:
                @pl.when(is_self)
                def _():
                    pltpu.make_async_copy(src, dst, recv).start()

                @pl.when(jnp.logical_not(is_self))
                def _():
                    copy.start()
                maybe.append(copy)
            else:
                copy.start()
                pending.append(copy)

    stride = heads // groups
    shift = lax.rem(part + groups * heads - 2 * head, groups)
    w_maybe = []
    for step in range(stride):
        offset = shift + groups * step
        which = lax.rem(head + offset, heads)
        copy = remote(w_in.at[which], wb.at[me], s_in.at[4, step], r_w.at[me], which * group + member)
        if step == 0:
            @pl.when(offset == 0)
            def _():
                pltpu.make_async_copy(w_in.at[which], wb.at[me], r_w.at[me]).start()

            @pl.when(offset != 0)
            def _():
                copy.start()
            w_maybe.append(copy)
        else:
            copy.start()
            pending.append(copy)
    spread(lambda w: kvq_in.at[w, 0], kv.at[heads + block_slot, 0], r_k.at[block_slot], 0)
    spread(lambda w: kvq_in.at[w, 1], kv.at[heads + block_slot, 1], r_v.at[block_slot], 1)
    spread(lambda w: step_in, stb.at[block_slot], r_st.at[block_slot], 2)
    spread(lambda w: kvq_in.at[w, 2], qb.at[block_slot], r_q.at[block_slot], 3)

    @pl.when(member == 0)
    def _():
        kv[:heads] = jnp.zeros((heads, 2, width, LANES), BF16)

    def landed(ref, sem):
        pltpu.make_async_copy(ref, ref, sem).wait()

    first = lax.rem(part + groups * heads - head, groups)
    for t in range(stride):
        slot = member + group * (first + groups * t)
        landed(wb.at[slot], r_w.at[slot])
        for other in range(groups):
            for d in range(group):
                if other + d == 0:
                    continue
                copy = remote(
                    wb.at[slot], wb.at[slot], s_wf.at[t, other * group + d], r_w.at[slot],
                    head * group + lax.rem(member + d, group), lax.rem(part + other, groups),
                )
                copy.start()
                pending.append(copy)

    forwards = []
    for i in range(heads):
        landed(kv.at[heads + i, 0], r_k.at[i])
        landed(kv.at[heads + i, 1], r_v.at[i])
        copy = remote(kv.at[heads + i], kv.at[i], s_kf.at[i], r_prior.at[i], me + 1)
        forwards.append(copy)

        @pl.when(member < group - 1)
        def _():
            copy.start()
    for d in range(group):
        for e in range(groups):
            if d + e == 0:
                continue
            for t in range(stride):
                slot = lax.rem(member + d, group) + group * (lax.rem(first + e, groups) + groups * t)
                landed(wb.at[slot], r_w.at[slot])
    for s in range(n):
        piece = wb[s].astype(F32)
        for m in range(3):
            wfull[m, s * rows : (s + 1) * rows, :] = piece[m * rows : (m + 1) * rows, :]
    for i in range(heads):
        landed(stb.at[i], r_st.at[i])

    w1 = wfull[0].astype(BF16)
    w3 = wfull[1].astype(BF16)
    w2 = wfull[2].astype(BF16)

    for i in range(heads):
        there = pl.ds(i * LANES, LANES)
        tgt[:, there] = (-stb[i, pl.ds(head, 1), :] * kv[heads + i, 1].astype(F32)).astype(BF16)
    chunk = 2 * LANES

    def grad_chunk(c, carry):
        there = pl.ds(pl.multiple_of(c * chunk, chunk), chunk)
        keys = jnp.concatenate([kv[heads + 2 * c, 0], kv[heads + 2 * c + 1, 0]], axis=1)
        gate = dot_tn(w1, keys) * scale
        up = dot_tn(w3, keys) * scale
        back = dot(w2, tgt[:, there]) * scale
        sigma = jax.nn.sigmoid(gate)
        silu = gate * sigma
        hid[:, there] = (silu * up).astype(BF16)
        gg[:, there] = (back * up * (sigma * (1.0 + gate * (1.0 - sigma)))).astype(BF16)
        gu[:, there] = (back * silu).astype(BF16)
        return carry

    lax.fori_loop(0, span // chunk, grad_chunk, 0)
    own_keys = jnp.concatenate([kv[heads + i, 0] for i in range(heads)], axis=1)
    for m, (left, right) in enumerate(((own_keys, gg), (own_keys, gu), (hid[...], tgt))):
        grad = dot_nt(left, right[...]) * scale
        for s in range(n):
            gstage[s % group, s // group, m * rows : (m + 1) * rows, :] = grad[s * rows : (s + 1) * rows, :]

    for d in range(1, group):
        other = lax.rem(member + d, group)
        copy = remote(
            gstage.at[other], ginc.at[d - 1], s_gp.at[d - 1], r_gp.at[d - 1], head * group + other
        )
        copy.start()
        pending.append(copy)

    @pl.when(member > 0)
    def _():
        for i in range(heads):
            landed(kv.at[i], r_prior.at[i])

    def flip(c, carry):
        at = pl.ds(pl.multiple_of(c * LANES, LANES), LANES)
        kn[at, :] = kv[c, 0].T
        return carry

    lax.fori_loop(0, 2 * heads, flip, 0)

    for d in range(1, group):
        landed(ginc.at[d - 1], r_gp.at[d - 1])
    sums[...] = jnp.zeros_like(sums)

    def add_up(i, carry):
        total = gstage[member, i]
        for d in range(1, group):
            total = total + ginc[d - 1, i]
        gsend[i] = total.astype(BF16)
        weight = wb[member + group * i].astype(F32)
        moved = weight - total
        for m in range(3):
            part = slice(m * rows, (m + 1) * rows)
            old = weight[part, :]
            new = moved[part, :]
            sums[m : m + 1, :] += jnp.sum(old * old, axis=0, keepdims=True)
            sums[4 + m : 5 + m, :] += jnp.sum(new * new, axis=0, keepdims=True)
        return carry

    lax.fori_loop(0, heads, add_up, 0)
    for d in range(1, group):
        copy = remote(
            sums, sinc.at[d - 1], s_sp.at[d - 1], r_sp.at[d - 1],
            head * group + lax.rem(member + d, group),
        )
        copy.start()
        pending.append(copy)


    for i in range(heads):
        landed(qb.at[i], r_q.at[i])

    reach = WINDOW + chunk
    key_at = lax.broadcasted_iota(jnp.int32, (reach, chunk), 0)
    query_at = lax.broadcasted_iota(jnp.int32, (reach, chunk), 1)
    distance = WINDOW + query_at - key_at
    in_window = (distance >= 0) & (distance < WINDOW)
    first_key = jnp.where(member == 0, span, 0)

    for h in range(heads):
        @pl.when(head == h)
        def _():
            at = slice(h * width, (h + 1) * width)
            gain_rows[0] = jnp.broadcast_to(fast_gain[:, at], (8, width))
            gain_rows[1] = jnp.broadcast_to(window_gain[:, at], (8, width))

    fast_column = gain_rows[0].T[:, 0:1]
    window_column = gain_rows[1].T[:, 0:1]

    def normalize(field, gain):
        mean_sq = jnp.mean(field * field, axis=0, keepdims=True)
        return field * lax.rsqrt(mean_sq + 1e-05) * gain

    outs = []

    def attend(turn):
        c = turn
        start = c * chunk
        query = jnp.concatenate([qb[2 * c], qb[2 * c + 1]], axis=1)
        scores = dot(kn[pl.ds(start, reach), :], query) * scale
        allowed = in_window & (key_at + start >= first_key)
        scores = jnp.where(allowed, scores, -1e30)
        weights = jnp.exp(scores - jnp.max(scores, axis=0, keepdims=True))
        probs = (weights / jnp.sum(weights, axis=0, keepdims=True)).astype(BF16)
        values = jnp.concatenate([kv[2 * c + i, 1] for i in range(reach // LANES)], axis=1)
        attended = dot(values, probs)
        window_part = normalize(attended, window_column)
        gate = dot_tn(w1, query) * scale
        up = dot_tn(w3, query) * scale
        hidden = (gate * jax.nn.sigmoid(gate) * up).astype(BF16)
        fast_part = normalize(dot_tn(w2, hidden) * scale, fast_column)
        result = (fast_part + window_part).astype(BF16)
        for half in range(2):
            i = 2 * c + half
            ostage[i] = result[:, half * LANES : (half + 1) * LANES]
            device = member * heads + i
            dst = out.at[head_rows(head), :]
            copy = remote(ostage.at[i], dst, s_o.at[i], r_o.at[head], device)
            outs.append((copy, device))

            @pl.when(device == me)
            def _():
                pltpu.make_async_copy(ostage.at[i], dst, r_o.at[head]).start()

            @pl.when(device != me)
            def _():
                copy.start()

    attend(0)
    for d in range(1, group):
        landed(sinc.at[d - 1], r_sp.at[d - 1])
    total = sums[...]
    for d in range(1, group):
        total = total + sinc[d - 1]
    scale_send[0:4, :] = jnp.sqrt((total[0:4] + 1e-06) / (total[4:8] + 1e-06))
    scale_send[4:8, :] = total[4:8]
    for step in range(heads):
        i = lax.rem(head + step, heads)
        device = member + group * i
        if step == 0:
            pltpu.make_async_copy(gsend.at[i], g_out.at[head], r_g.at[head]).start()
            pltpu.make_async_copy(scale_send, scale_out.at[head], r_sc.at[head]).start()
        else:
            copy = remote(gsend.at[i], g_out.at[head], s_g.at[step], r_g.at[head], device)
            copy.start()
            pending.append(copy)
            copy = remote(scale_send, scale_out.at[head], s_sc.at[step], r_sc.at[head], device)
            copy.start()
            pending.append(copy)
    for c in range(1, span // chunk):
        attend(c)

    for i in range(heads):
        landed(g_out.at[i], r_g.at[i])
        landed(scale_out.at[i], r_sc.at[i])
        landed(out.at[pl.ds(i * width, width), :], r_o.at[i])
    for copy in pending:
        copy.wait_send()

    @pl.when(jnp.logical_not(is_self))
    def _():
        for copy in maybe:
            copy.wait_send()

    @pl.when(shift != 0)
    def _():
        for copy in w_maybe:
            copy.wait_send()

    @pl.when(member < group - 1)
    def _():
        for copy in forwards:
            copy.wait_send()
    for copy, device in outs:
        @pl.when(device != me)
        def _():
            copy.wait_send()


def prepare(heads, width, rows, k, v, q, weights, kvq, pieces, wide):
    for m, ref in enumerate((k, v, q)):
        flipped = ref[...].T
        for h in range(heads):
            kvq[h, m] = flipped[h * width : (h + 1) * width]
    for h in range(heads):
        for m in range(3):
            at = (m * heads + h) * width
            wide[h, m * rows : (m + 1) * rows, :] = weights[:, at : at + width]
        pieces[h] = wide[h].astype(BF16)


def finish(heads, width, rows, out_t, grads, scales, weights, layer_out, new_weights, momentum):
    layer_out[...] = out_t[...].T
    for h in range(heads):
        grad = grads[h].astype(F32)
        for m in range(3):
            at = (m * heads + h) * width
            part = grad[m * rows : (m + 1) * rows, :]
            momentum[:, at : at + width] = part
            new_weights[:, at : at + width] = (weights[:, at : at + width] - part) * scales[h, m : m + 1, :]


def shards(queries, key_vectors, value_vectors, step_sizes, fast_weights, fast_gain, window_gain):
    tokens = queries.shape[0]
    heads = step_sizes.shape[1]
    width = queries.shape[1] // heads
    n = lax.axis_size("seq")
    groups = lax.axis_size("groups")
    group = n // heads
    rows = width // n
    assert tokens == LANES and heads * tokens == WINDOW
    span = heads * LANES
    vmem = pl.BlockSpec(memory_space=pltpu.VMEM)
    dma = pltpu.SemaphoreType.DMA
    more = max(group - 1, 1)
    kvq, pieces = pl.pallas_call(
        functools.partial(prepare, heads, width, rows),
        out_shape=(
            jax.ShapeDtypeStruct((heads, 3, width, LANES), BF16),
            jax.ShapeDtypeStruct((heads, 3 * rows, width), BF16),
        ),
        in_specs=[vmem] * 4,
        out_specs=(vmem, vmem),
        scratch_shapes=[pltpu.VMEM((heads, 3 * rows, width), F32)],
        name="prepare",
    )(key_vectors, value_vectors, queries, fast_weights)
    out_t, grads, scales = pl.pallas_call(
        functools.partial(kernel, n, groups, heads, width),
        out_shape=(
            jax.ShapeDtypeStruct((heads * width, LANES), BF16),
            jax.ShapeDtypeStruct((heads, 3 * rows, width), BF16),
            jax.ShapeDtypeStruct((heads, 8, width), F32),
        ),
        in_specs=[vmem] * 5,
        out_specs=(vmem, vmem, vmem),
        scratch_shapes=[
            pltpu.VMEM((2 * heads, 2, width, LANES), BF16),
            pltpu.VMEM((heads, width, LANES), BF16),
            pltpu.VMEM((heads, heads, LANES), F32),
            pltpu.VMEM((n, 3 * rows, width), BF16),
            pltpu.VMEM((3, width, width), F32),
            pltpu.VMEM((2 * span, width), BF16),
            pltpu.VMEM((width, span), BF16),
            pltpu.VMEM((width, span), BF16),
            pltpu.VMEM((width, span), BF16),
            pltpu.VMEM((width, span), BF16),
            pltpu.VMEM((group, heads, 3 * rows, width), F32),
            pltpu.VMEM((more, heads, 3 * rows, width), F32),
            pltpu.VMEM((heads, 3 * rows, width), BF16),
            pltpu.VMEM((8, width), F32),
            pltpu.VMEM((more, 8, width), F32),
            pltpu.VMEM((8, width), F32),
            pltpu.VMEM((heads, width, LANES), BF16),
            pltpu.VMEM((2, 8, width), F32),
            dma((5, heads)), dma((heads,)), dma((heads,)), dma((heads,)), dma((heads,)), dma((heads,)), dma((n,)),
            dma((heads // groups, groups * group)), dma((heads,)),
            dma((more,)), dma((more,)), dma((more,)), dma((more,)),
            dma((heads,)), dma((heads,)), dma((heads,)), dma((heads,)), dma((heads,)), dma((heads,)),
        ],
        compiler_params=pltpu.CompilerParams(
            collective_id=0, has_side_effects=True, vmem_limit_bytes=60 << 20
        ),
        name="ttt",
    )(kvq, step_sizes.T, pieces, fast_gain.reshape(1, -1), window_gain.reshape(1, -1))
    return pl.pallas_call(
        functools.partial(finish, heads, width, rows),
        out_shape=(
            jax.ShapeDtypeStruct(queries.shape, BF16),
            jax.ShapeDtypeStruct(fast_weights.shape, F32),
            jax.ShapeDtypeStruct(fast_weights.shape, F32),
        ),
        in_specs=[vmem] * 4,
        out_specs=(vmem, vmem, vmem),
        name="finish",
    )(out_t, grads, scales, fast_weights)


def solution(mesh):
    in_specs = (
        P(("groups", "seq"), None),
        P(("groups", "seq"), None),
        P(("groups", "seq"), None),
        P(("groups", "seq"), None),
        P("seq", None),
        P(),
        P(),
    )
    out_specs = (P(("groups", "seq"), None), P(("groups", "seq"), None), P(("groups", "seq"), None))
    return jax.shard_map(shards, mesh=mesh, in_specs=in_specs, out_specs=out_specs, check_vma=False)
```
